32 devices in a mesh: mem: 4 (over x, core), row: 4 (over z), col: 2 (over y).
Axes of the slice: x: 2, y: 2, z: 4, core: 2. Of those that a mesh axis runs over, the one named last changes fastest.
Arguments:
- fields: bfloat16 [16, 16, 64, 256], P('mem', 'row', 'col'), may hold values from -6 to 6
- norm_gain: float32 [256], replicated, may hold values from 0.5 to 1.5
- w_query: bfloat16 [256, 256], replicated, may hold values from -11 to 11
- w_key: bfloat16 [256, 256], replicated, may hold values from -6 to 6
- w_value: bfloat16 [256, 256], replicated, may hold values from -0.375 to 0.375
- w_out: bfloat16 [256, 256], replicated, may hold values from -0.375 to 0.375
- mix_kernel: float32 [3, 3, 256], replicated, may hold values from -1.5 to 1.5
- cotangent: bfloat16 [16, 16, 64, 256], P('mem', 'row', 'col'), may hold values from -6 to 6
Outputs:
- grad_fields: bfloat16 [16, 16, 64, 256], P('mem', 'row', 'col')
- grad_gain: float32 [256], replicated
- grad_query: float32 [256, 256], replicated
- grad_key: float32 [256, 256], replicated
- grad_value: float32 [256, 256], replicated
- grad_out: float32 [256, 256], replicated
- grad_kernel: float32 [3, 3, 256], replicated
The draws below stay inside these ranges and needn't reach their ends.
All inputs are finite; a program needn't handle non-finite values.
Results may differ from the reference program's by a relative error of at most 0.015.
The reference program's roundings to bfloat16 on the way count: a program that leaves them out, or rounds other values in their place, can miss the bound.
Values may be sent and summed in bfloat16 or wider, within the bound.
A program may use at most 64 MiB of HBM per device.

```python
import math
import jax
import jax.numpy as jnp
from jax import lax

D = 256
HEADS = 8
MEM_DEV = 4
MEMBERS = 16
NR = 16
NC = 64


def shared_basis(key):
    return jnp.clip(jax.random.normal(jax.random.fold_in(key, 11), (D, D), jnp.float32), -4.0, 4.0)


def draw_w_query(key, part):
    jitter = jnp.clip(jax.random.normal(jax.random.fold_in(key, 12), (D, D), jnp.float32), -4.0, 4.0)
    mixed = jitter
    return (mixed / math.sqrt(D)).astype(jnp.bfloat16)


def draw_w_key(key, part):
    basis = shared_basis(key)
    mixed = basis
    return (mixed / math.sqrt(D)).astype(jnp.bfloat16)


def block_scale(own_key, shape, pieces, smallest, high):
    def one(position, parts):
        heights = jax.random.uniform(jax.random.fold_in(jax.random.fold_in(own_key, 6), position), (parts,), jnp.float32, smallest / len(pieces), high / len(pieces))
        return jnp.repeat(jnp.exp(heights), shape[position] // parts).reshape((-1,) + (1,) * (len(shape) - position - 1))

    loudness = one(*pieces[0])
    for cut in pieces[1:]:
        loudness = loudness * one(*cut)
    return loudness


def normal_values(own_key, dims, scale, bound, split=(), kind=jnp.bfloat16):
    values = scale * jax.random.normal(own_key, dims, jnp.float32)
    if split:
        values = values * block_scale(own_key, dims, split, -0.22, 0.18)
    return jnp.clip(values, -bound, bound).astype(kind)


def setup_inputs(seed: int = 0) -> dict:
    key_list = jax.random.split(jax.random.key(seed), 9)
    fields = normal_values(key_list[0], (MEMBERS, NR, NC, D), 1.0, 6.0, ((0, 4), (1, 4), (2, 2)))
    norm_gain = jnp.clip(1.0 + 0.1 * jax.random.normal(key_list[1], (D,), jnp.float32), 0.5, 1.5)
    w_query = draw_w_query(jax.random.fold_in(key_list[8], 71), 0)
    w_key = draw_w_key(jax.random.fold_in(key_list[8], 71), 0)
    w_value = normal_values(key_list[4], (D, D), D ** -0.5, 0.375)
    w_out = normal_values(key_list[5], (D, D), D ** -0.5, 0.375)
    mix_kernel = normal_values(key_list[6], (3, 3, D), 0.3, 1.5, (), jnp.float32)
    cotangent = normal_values(key_list[7], (MEMBERS, NR, NC, D), 1.0, 6.0, ((0, 4), (1, 4), (2, 2)))
    return dict(fields=fields, norm_gain=norm_gain, w_query=w_query, w_key=w_key, w_value=w_value, w_out=w_out, mix_kernel=mix_kernel, cotangent=cotangent)


epsilon = 1e-06

def project(values, weight):
    shape = values.shape
    flat_in = values.reshape(-1, shape[-1])
    return jnp.dot(flat_in, weight, preferred_element_type=jnp.float32).reshape(shape[:-1] + (weight.shape[1],))

def reference(fields, norm_gain, w_query, w_key, w_value, w_out, mix_kernel, cotangent):
    members_all, grid_rows, grid_cols, model_width = fields.shape
    head_dim = model_width // HEADS
    score_scale = 1.0 / math.sqrt(head_dim)
    group_count = members_all // MEM_DEV
    padded_cot = jnp.pad(cotangent, ((0, 0), (1, 1), (1, 1), (0, 0)))
    summed = jnp.zeros(fields.shape, jnp.float32)
    for row_off in range(3):
        for col_off in range(3):
            summed = summed + mix_kernel[row_off, col_off] * padded_cot[:, 2 - row_off:2 - row_off + grid_rows, 2 - col_off:2 - col_off + grid_cols, :].astype(jnp.float32)
    grad_mixed_all = summed.astype(jnp.bfloat16)

    def attend_row(running, row_in):
        row_fields, row_grad_mixed, row_cot = row_in
        col_count = row_fields.shape[1]
        flat_in = row_fields.astype(jnp.float32)
        inv_rms = lax.rsqrt(lax.optimization_barrier(jnp.mean(flat_in * flat_in, axis=-1, keepdims=True)) + epsilon)
        normed = flat_in * inv_rms
        inputs = (normed * norm_gain).astype(jnp.bfloat16)
        queries = project(inputs, w_query).astype(jnp.bfloat16)
        key_proj = project(inputs, w_key).astype(jnp.bfloat16)
        value_proj = project(inputs, w_value).astype(jnp.bfloat16)
        head_shape = (members_all, col_count, HEADS, head_dim)
        query_heads = queries.reshape(head_shape).astype(jnp.float32)
        key_heads = key_proj.reshape(head_shape).astype(jnp.float32)
        value_heads = value_proj.reshape(head_shape).astype(jnp.float32)
        scores = jnp.einsum('mche,nche->chmn', query_heads, key_heads) * score_scale
        row_max = lax.optimization_barrier(jnp.max(scores, axis=-1, keepdims=True))
        lifted = jnp.exp(scores - row_max)
        attn_prob = lifted / lax.optimization_barrier(jnp.sum(lifted, axis=-1, keepdims=True))
        prob_b = attn_prob.astype(jnp.bfloat16).astype(jnp.float32)
        attended = jnp.einsum('chmn,nche->mche', prob_b, value_heads).astype(jnp.bfloat16)
        attended = attended.reshape(members_all, col_count, model_width)
        mixed_row = project(attended, w_out).astype(jnp.bfloat16)
        grad_att = project(row_grad_mixed, w_out.T).astype(jnp.bfloat16)
        grad_heads = grad_att.reshape(head_shape).astype(jnp.float32)
        grad_prob = jnp.einsum('mche,nche->chmn', grad_heads, value_heads)
        inner = lax.optimization_barrier(jnp.sum(attn_prob * grad_prob, axis=-1, keepdims=True))
        grad_score = (attn_prob * (grad_prob - inner) * score_scale).astype(jnp.bfloat16).astype(jnp.float32)
        grad_q = jnp.einsum('chmn,nche->mche', grad_score, key_heads).astype(jnp.bfloat16)
        score_groups = grad_score.reshape(col_count, HEADS, group_count, MEM_DEV, members_all)
        prob_groups = prob_b.reshape(col_count, HEADS, group_count, MEM_DEV, members_all)
        query_groups = query_heads.reshape(group_count, MEM_DEV, col_count, HEADS, head_dim)
        grad_groups = grad_heads.reshape(group_count, MEM_DEV, col_count, HEADS, head_dim)
        part_k = lax.optimization_barrier(jnp.einsum('chgmn,gmche->gnche', score_groups, query_groups).astype(jnp.bfloat16))
        part_v = lax.optimization_barrier(jnp.einsum('chgmn,gmche->gnche', prob_groups, grad_groups).astype(jnp.bfloat16))
        grad_k = lax.optimization_barrier(jnp.sum(part_k.astype(jnp.float32), axis=0)).astype(jnp.bfloat16)
        grad_v = lax.optimization_barrier(jnp.sum(part_v.astype(jnp.float32), axis=0)).astype(jnp.bfloat16)
        flat_shape = (members_all * col_count, model_width)
        grad_q2 = grad_q.reshape(flat_shape)
        grad_k2 = grad_k.reshape(flat_shape)
        grad_v2 = grad_v.reshape(flat_shape)
        inputs2 = inputs.reshape(flat_shape)
        grad_in = jnp.dot(grad_q2, w_query.T, preferred_element_type=jnp.float32) + jnp.dot(grad_k2, w_key.T, preferred_element_type=jnp.float32) + jnp.dot(grad_v2, w_value.T, preferred_element_type=jnp.float32)
        normed2 = normed.reshape(flat_shape)
        grad_normed = grad_in * norm_gain
        inv2 = inv_rms.reshape(-1, 1)
        grad_row = row_cot.reshape(flat_shape).astype(jnp.float32) + inv2 * (grad_normed - normed2 * lax.optimization_barrier(jnp.mean(grad_normed * normed2, axis=-1, keepdims=True)))
        acc_q, acc_k, acc_v, acc_out, acc_gain = running
        acc_q = acc_q + jnp.dot(inputs2.T, grad_q2, preferred_element_type=jnp.float32)
        acc_k = acc_k + jnp.dot(inputs2.T, grad_k2, preferred_element_type=jnp.float32)
        acc_v = acc_v + jnp.dot(inputs2.T, grad_v2, preferred_element_type=jnp.float32)
        acc_out = acc_out + jnp.dot(attended.reshape(flat_shape).T, row_grad_mixed.reshape(flat_shape), preferred_element_type=jnp.float32)
        acc_gain = acc_gain + lax.optimization_barrier(jnp.sum(grad_in * normed2, axis=0))
        outputs = (mixed_row, grad_row.astype(jnp.bfloat16).reshape(members_all, col_count, model_width))
        return ((acc_q, acc_k, acc_v, acc_out, acc_gain), outputs)
    square = jnp.zeros((model_width, model_width), jnp.float32)
    start = (square, square, square, square, jnp.zeros((model_width,), jnp.float32))
    row_inputs = (jnp.moveaxis(fields, 1, 0), jnp.moveaxis(grad_mixed_all, 1, 0), jnp.moveaxis(cotangent, 1, 0))
    running, outputs = lax.scan(attend_row, start, row_inputs)
    mixed_all = jnp.moveaxis(outputs[0], 0, 1)
    grad_fields = jnp.moveaxis(outputs[1], 0, 1)
    scale_all = 1.0 / math.sqrt(members_all * grid_rows * grid_cols)
    kernel_terms = []
    padded_mixed = jnp.pad(mixed_all, ((0, 0), (1, 1), (1, 1), (0, 0)))
    for row_off in range(3):
        for col_off in range(3):
            shifted = padded_mixed[:, row_off:row_off + grid_rows, col_off:col_off + grid_cols, :].astype(jnp.float32)
            kernel_terms.append(lax.optimization_barrier(jnp.sum(shifted * cotangent.astype(jnp.float32), axis=(0, 1, 2))))
    grad_kernel = jnp.stack(kernel_terms).reshape(3, 3, model_width) * scale_all
    acc_q, acc_k, acc_v, acc_out, acc_gain = running
    return (grad_fields, acc_gain * scale_all, acc_q * scale_all, acc_k * scale_all, acc_v * scale_all, acc_out * scale_all, grad_kernel)
```

```python
import functools
import math

import jax
import jax.numpy as jnp
from jax import lax
from jax.experimental import pallas as pl
from jax.experimental.pallas import tpu as pltpu
from jax.sharding import PartitionSpec as P

HEADS = 8
SUB = 8

epsilon = 1e-06
F32 = jnp.float32
BF16 = jnp.bfloat16


def dot_nn(a, b):
    return lax.dot_general(a, b, (((1,), (0,)), ((), ())), preferred_element_type=F32)


def dot_nt(a, b):
    return lax.dot_general(a, b, (((1,), (1,)), ((), ())), preferred_element_type=F32)


def flip(x):
    return x.astype(F32).T.astype(x.dtype)


def to_groups(x):
    members, cells, width = x.shape
    return jnp.concatenate(
        [x[:, i : i + SUB, :].reshape(members * SUB, width) for i in range(0, cells, SUB)], axis=0
    )


def from_groups(x, members, cells):
    width = x.shape[-1]
    size = members * SUB
    return jnp.concatenate(
        [x[g * size : (g + 1) * size].reshape(members, SUB, width) for g in range(cells // SUB)],
        axis=1,
    )


def attend_group(keys, vals, q_t, ga_t, k_t, v_t):
    tokens, width = keys.shape
    members = tokens // SUB
    head_dim = width // HEADS
    scale = 1.0 / math.sqrt(head_dim)
    head_of = lax.broadcasted_iota(jnp.int32, (tokens, width), 1) // head_dim
    row_cell = lax.broadcasted_iota(jnp.int32, (SUB, tokens), 0)
    col_cell = lax.broadcasted_iota(jnp.int32, (SUB, tokens), 1) % SUB
    same = (row_cell == col_cell)[None]
    outs = ([], [], [], [])
    for h in range(HEADS):
        own = head_of == h
        hs = slice(h * head_dim, (h + 1) * head_dim)
        k_own = jnp.where(own, keys.astype(F32), 0.0).astype(BF16)
        v_own = jnp.where(own, vals.astype(F32), 0.0).astype(BF16)
        scores = dot_nn(k_own, q_t).reshape(members, SUB, tokens) * scale
        grad_prob = dot_nn(v_own, ga_t).reshape(members, SUB, tokens)
        lifted = jnp.exp(scores - jnp.max(scores, axis=0, keepdims=True))
        prob = lifted * (1.0 / jnp.sum(lifted, axis=0, keepdims=True))
        inner = jnp.sum(prob * grad_prob, axis=0, keepdims=True)
        grad_score = prob * (grad_prob - inner) * scale
        prob_b = jnp.where(same, prob, 0.0).reshape(tokens, tokens).astype(BF16)
        gs_b = jnp.where(same, grad_score, 0.0).reshape(tokens, tokens).astype(BF16)
        outs[0].append(dot_nn(v_t[hs], prob_b))
        outs[1].append(dot_nn(k_t[hs], gs_b))
        outs[2].append(dot_nt(q_t[hs], gs_b))
        outs[3].append(dot_nt(ga_t[hs], prob_b))
    return tuple(jnp.concatenate(o, axis=0).astype(BF16) for o in outs)


def block_kernel(
    f_ref, gm_ref, gain_ref, wq_ref, wk_ref, wv_ref, wo_ref,
    corr_ref, mixed_ref, grads_ref, gain_out_ref,
):
    members, cells, width = f_ref.shape
    size = members * SUB
    flat = to_groups(f_ref[...].astype(F32))
    gm = to_groups(gm_ref[...].astype(F32)).astype(BF16)
    wq, wk, wv, wo = (w[...] for w in (wq_ref, wk_ref, wv_ref, wo_ref))
    inv = lax.rsqrt(jnp.mean(flat * flat, axis=-1, keepdims=True) + epsilon)
    normed = flat * inv
    inputs = (normed * gain_ref[...]).astype(BF16)
    in_t = flip(inputs)
    keys = dot_nn(inputs, wk).astype(BF16)
    vals = dot_nn(inputs, wv).astype(BF16)
    q_t = dot_nn(flip(wq), in_t).astype(BF16)
    k_t = dot_nn(flip(wk), in_t).astype(BF16)
    v_t = dot_nn(flip(wv), in_t).astype(BF16)
    ga_t = dot_nt(wo, gm).astype(BF16)
    parts = []
    for g in range(cells // SUB):
        rows = slice(g * size, (g + 1) * size)
        parts.append(
            attend_group(
                keys[rows], vals[rows], q_t[:, rows], ga_t[:, rows], k_t[:, rows], v_t[:, rows]
            )
        )
    att_t, gq_t, gk_t, gv_t = (jnp.concatenate(p, axis=1) for p in zip(*parts))
    mixed = dot_nn(flip(att_t), wo)
    mixed_ref[...] = from_groups(mixed, members, cells).astype(BF16)
    grad_in = (dot_nn(wq, gq_t) + dot_nn(wk, gk_t) + dot_nn(wv, gv_t)).T
    grads_ref[0:width] = dot_nt(in_t, gq_t)
    grads_ref[width : 2 * width] = dot_nt(in_t, gk_t)
    grads_ref[2 * width : 3 * width] = dot_nt(in_t, gv_t)
    grads_ref[3 * width : 4 * width] = dot_nn(att_t, gm)
    gain_out_ref[...] = jnp.sum(grad_in * normed, axis=0, keepdims=True)
    grad_normed = grad_in * gain_ref[...]
    corr = inv * (grad_normed - normed * jnp.mean(grad_normed * normed, axis=-1, keepdims=True))
    corr_ref[...] = from_groups(corr, members, cells).astype(BF16)


def block(f, gm, gain, wq, wk, wv, wo, interpret=False):
    width = f.shape[-1]
    return pl.pallas_call(
        block_kernel,
        out_shape=(
            jax.ShapeDtypeStruct(f.shape, BF16),
            jax.ShapeDtypeStruct(f.shape, BF16),
            jax.ShapeDtypeStruct((4 * width, width), F32),
            jax.ShapeDtypeStruct((1, width), F32),
        ),
        interpret=interpret,
        compiler_params=pltpu.CompilerParams(vmem_limit_bytes=48 * 2**20),
    )(f, gm, gain.reshape(1, -1), wq, wk, wv, wo)


def with_halo(x, sides, width):
    for axis, dim in sides:
        size, length = (lax.axis_size(axis), x.shape[dim])
        up = [(i, (i + 1) % size) for i in range(size - 1)]
        down = [(j, i) for i, j in up]
        last = lax.slice_in_dim(x, length - width, length, axis=dim)
        first = lax.slice_in_dim(x, 0, width, axis=dim)
        before = lax.ppermute(last, axis, up)
        after = lax.ppermute(first, axis, down)
        x = jnp.concatenate([before, x, after], axis=dim)
    return x


def local(fields, norm_gain, w_query, w_key, w_value, w_out, mix_kernel, cotangent):
    members, tile_rows, tile_cols, width = fields.shape
    cells = tile_rows * tile_cols
    padded_cot = with_halo(cotangent, (("row", 1), ("col", 2)), 1)
    shifts = [
        padded_cot[:, 2 - i : 2 - i + tile_rows, 2 - j : 2 - j + tile_cols, :].astype(F32)
        for i in range(3)
        for j in range(3)
    ]
    taps = mix_kernel.reshape(9, width)
    summed = jnp.zeros(fields.shape, F32)
    for i in range(9):
        summed = summed + taps[i] * shifts[i]
    flat = (members, cells, width)
    sent = jnp.stack([fields.reshape(flat), summed.astype(BF16).reshape(flat)])
    got = lax.all_to_all(sent, "mem", split_axis=2, concat_axis=1, tiled=True)
    corr, mixed, grads, gain = block(got[0], got[1], norm_gain, w_query, w_key, w_value, w_out)
    back = lax.all_to_all(jnp.stack([corr, mixed]), "mem", split_axis=1, concat_axis=2, tiled=True)
    grad_fields = (cotangent.astype(F32) + back[0].reshape(fields.shape).astype(F32)).astype(BF16)
    mixed = back[1].reshape(fields.shape).astype(F32)
    terms = jnp.stack([jnp.sum(s * mixed, axis=(0, 1, 2)) for s in shifts])
    total = lax.psum(jnp.concatenate([grads, gain, terms]), ("mem", "row", "col"))
    tokens = math.prod(fields.shape[:3]) * math.prod(
        lax.axis_size(a) for a in ("mem", "row", "col")
    )
    total = total * (1.0 / math.sqrt(tokens))
    w = [total[i * width : (i + 1) * width] for i in range(4)]
    return (grad_fields, total[4 * width], *w, total[4 * width + 1 :].reshape(3, 3, width))


def solution(mesh):
    tile = P("mem", "row", "col", None)
    in_specs = (tile, P(), P(), P(), P(), P(), P(), tile)
    out_specs = (tile, P(), P(), P(), P(), P(), P())
    return jax.shard_map(local, mesh=mesh, in_specs=in_specs, out_specs=out_specs, check_vma=False)
```

```python
import functools
import math

import jax
import jax.numpy as jnp
from jax import lax
from jax.experimental import pallas as pl
from jax.experimental.pallas import tpu as pltpu
from jax.sharding import PartitionSpec as P

HEADS = 8
SUB = 8

epsilon = 1e-06
F32 = jnp.float32
BF16 = jnp.bfloat16


def dot_nn(a, b):
    return lax.dot_general(a, b, (((1,), (0,)), ((), ())), preferred_element_type=F32)


def dot_nt(a, b):
    return lax.dot_general(a, b, (((1,), (1,)), ((), ())), preferred_element_type=F32)


def flip(x):
    return x.astype(F32).T.astype(x.dtype)


def to_groups(x):
    members, cells, width = x.shape
    return jnp.concatenate(
        [x[:, i : i + SUB, :].reshape(members * SUB, width) for i in range(0, cells, SUB)], axis=0
    )


def from_groups(x, members, cells):
    width = x.shape[-1]
    size = members * SUB
    return jnp.concatenate(
        [x[g * size : (g + 1) * size].reshape(members, SUB, width) for g in range(cells // SUB)],
        axis=1,
    )


def attend_group(keys, vals, q_t, ga_t, k_t, v_t):
    tokens, width = keys.shape
    members = tokens // SUB
    head_dim = width // HEADS
    scale = 1.0 / math.sqrt(head_dim)
    head_of = lax.broadcasted_iota(jnp.int32, (tokens, width), 1) // head_dim
    row_cell = lax.broadcasted_iota(jnp.int32, (SUB, tokens), 0)
    col_cell = lax.broadcasted_iota(jnp.int32, (SUB, tokens), 1) % SUB
    same = (row_cell == col_cell)[None]
    outs = ([], [], [], [])
    for h in range(HEADS):
        own = head_of == h
        hs = slice(h * head_dim, (h + 1) * head_dim)
        k_own = jnp.where(own, keys.astype(F32), 0.0).astype(BF16)
        v_own = jnp.where(own, vals.astype(F32), 0.0).astype(BF16)
        scores = dot_nn(k_own, q_t).reshape(members, SUB, tokens) * scale
        grad_prob = dot_nn(v_own, ga_t).reshape(members, SUB, tokens)
        lifted = jnp.exp(scores - jnp.max(scores, axis=0, keepdims=True))
        prob = lifted * (1.0 / jnp.sum(lifted, axis=0, keepdims=True))
        inner = jnp.sum(prob * grad_prob, axis=0, keepdims=True)
        grad_score = prob * (grad_prob - inner) * scale
        prob_b = jnp.where(same, prob, 0.0).reshape(tokens, tokens).astype(BF16)
        gs_b = jnp.where(same, grad_score, 0.0).reshape(tokens, tokens).astype(BF16)
        outs[0].append(dot_nn(v_t[hs], prob_b))
        outs[1].append(dot_nn(k_t[hs], gs_b))
        outs[2].append(dot_nt(q_t[hs], gs_b))
        outs[3].append(dot_nt(ga_t[hs], prob_b))
    return tuple(jnp.concatenate(o, axis=0).astype(BF16) for o in outs)


def block_kernel(
    f_ref, gm_ref, gain_ref, wq_ref, wk_ref, wv_ref, wo_ref,
    corr_ref, mixed_ref, grads_ref, gain_out_ref,
):
    members, cells, width = f_ref.shape
    size = members * SUB
    flat = to_groups(f_ref[...].astype(F32))
    gm = to_groups(gm_ref[...].astype(F32)).astype(BF16)
    wq, wk, wv, wo = (w[...] for w in (wq_ref, wk_ref, wv_ref, wo_ref))
    inv = lax.rsqrt(jnp.mean(flat * flat, axis=-1, keepdims=True) + epsilon)
    normed = flat * inv
    inputs = (normed * gain_ref[...]).astype(BF16)
    in_t = flip(inputs)
    keys = dot_nn(inputs, wk).astype(BF16)
    vals = dot_nn(inputs, wv).astype(BF16)
    q_t = dot_nn(flip(wq), in_t).astype(BF16)
    k_t = dot_nn(flip(wk), in_t).astype(BF16)
    v_t = dot_nn(flip(wv), in_t).astype(BF16)
    ga_t = dot_nt(wo, gm).astype(BF16)
    parts = []
    for g in range(cells // SUB):
        rows = slice(g * size, (g + 1) * size)
        parts.append(
            attend_group(
                keys[rows], vals[rows], q_t[:, rows], ga_t[:, rows], k_t[:, rows], v_t[:, rows]
            )
        )
    att_t, gq_t, gk_t, gv_t = (jnp.concatenate(p, axis=1) for p in zip(*parts))
    mixed = dot_nn(flip(att_t), wo)
    mixed_ref[...] = from_groups(mixed, members, cells).astype(BF16)
    grad_in = (dot_nn(wq, gq_t) + dot_nn(wk, gk_t) + dot_nn(wv, gv_t)).T
    grads_ref[0:width] = dot_nt(in_t, gq_t)
    grads_ref[width : 2 * width] = dot_nt(in_t, gk_t)
    grads_ref[2 * width : 3 * width] = dot_nt(in_t, gv_t)
    grads_ref[3 * width : 4 * width] = dot_nn(att_t, gm)
    gain_out_ref[...] = jnp.sum(grad_in * normed, axis=0, keepdims=True)
    grad_normed = grad_in * gain_ref[...]
    corr = inv * (grad_normed - normed * jnp.mean(grad_normed * normed, axis=-1, keepdims=True))
    corr_ref[...] = from_groups(corr, members, cells).astype(BF16)


def block(f, gm, gain, wq, wk, wv, wo, interpret=False):
    width = f.shape[-1]
    return pl.pallas_call(
        block_kernel,
        out_shape=(
            jax.ShapeDtypeStruct(f.shape, BF16),
            jax.ShapeDtypeStruct(f.shape, BF16),
            jax.ShapeDtypeStruct((4 * width, width), F32),
            jax.ShapeDtypeStruct((1, width), F32),
        ),
        interpret=interpret,
        compiler_params=pltpu.CompilerParams(vmem_limit_bytes=48 * 2**20),
    )(f, gm, gain.reshape(1, -1), wq, wk, wv, wo)


MESH = pl.DeviceIdType.MESH
VMEM_SPEC = pl.BlockSpec(memory_space=pltpu.VMEM)


def enter(peers):
    barrier = pltpu.get_barrier_semaphore()
    for peer in peers:
        pl.semaphore_signal(barrier, inc=1, device_id=peer, device_id_type=MESH)
    pl.semaphore_wait(barrier, len(peers))


def push(src, dst, send_sem, recv_sem, peer):
    return pltpu.make_async_remote_copy(
        src_ref=src, dst_ref=dst, send_sem=send_sem, recv_sem=recv_sem,
        device_id=peer, device_id_type=MESH,
    )


def exchange_kernel(count, inward, *refs):
    srcs, dsts, (send, recv) = refs[:2], refs[2:4], refs[4:]
    me = lax.axis_index("mem")
    row, col = lax.axis_index("row"), lax.axis_index("col")
    others = [lax.rem(me + k, count) for k in range(1, count)]
    enter([(o, row, col) for o in others])

    def view(ref, i, by_chunk):
        return ref.at[:, i] if by_chunk else ref.at[i]

    copies = []
    for t in range(2):
        for o in others:
            copy = push(
                view(srcs[t], o, inward), view(dsts[t], me, not inward),
                send.at[t, o], recv.at[t, me], (o, row, col),
            )
            copy.start()
            copies.append(copy)
    for t in range(2):
        if inward:
            dsts[t][me] = srcs[t][:, me]
        else:
            dsts[t][:, me] = srcs[t][me]
    for copy in copies:
        copy.wait_send()
    for t in range(2):
        for o in others:
            push(
                view(srcs[t], o, inward), view(dsts[t], o, not inward),
                send.at[t, o], recv.at[t, o], (o, row, col),
            ).wait_recv()


def exchange(a, b, inward, collective_id):
    count = lax.axis_size("mem")
    shape = a.shape
    out = (shape[1], shape[0]) + shape[2:]
    return pl.pallas_call(
        functools.partial(exchange_kernel, count, inward),
        out_shape=(jax.ShapeDtypeStruct(out, a.dtype),) * 2,
        in_specs=[VMEM_SPEC] * 2,
        out_specs=(VMEM_SPEC,) * 2,
        scratch_shapes=[pltpu.SemaphoreType.DMA((2, count))] * 2,
        compiler_params=pltpu.CompilerParams(collective_id=collective_id, has_side_effects=True),
    )(a, b)


def sum_kernel(
    planes, rows, cols, scale,
    g_ref, s_ref, out_ref, sout_ref,
    a_src, a_dst, acc1, b_src, b_dst, acc2, c_src, c_dst, gz, gp, ga, s_a, s_b, s_c,
    send_a, recv_a, send_b, recv_b, send_c, recv_c,
    send_z, recv_z, send_p, recv_p, send_g, recv_g,
    ssend_b, srecv_b, ssend_c, srecv_c, ssend_a, srecv_a,
):
    mem, row, col = (lax.axis_index(a) for a in ("mem", "row", "col"))
    core = lax.rem(mem, 2)
    other = 1 - core
    me_p = lax.div(mem, 2) * cols + col
    partner = (mem + 1 - 2 * core, row, col)

    def plane_peer(p):
        return (lax.div(p, cols) * 2 + core, row, lax.rem(p, cols))

    plane_others = [lax.rem(me_p + k, planes) for k in range(1, planes)]
    row_others = [lax.rem(row + k, rows) for k in range(1, rows)]
    enter(
        [partner]
        + [plane_peer(p) for p in plane_others]
        + [(mem, r, col) for r in row_others]
    )

    a_src[...] = g_ref[other].astype(BF16)
    first = push(a_src, a_dst, send_a, recv_a, partner)
    first.start()
    s_a[core] = s_ref[...]
    small = push(s_a.at[core], s_a.at[core], ssend_a, srecv_a, partner)
    small.start()
    first.wait()
    acc1[...] = g_ref[core] + a_dst[...].astype(F32)
    b_src[...] = acc1[...].astype(BF16)

    sent = []
    for p in plane_others:
        copy = push(b_src.at[p], b_dst.at[me_p], send_b.at[p], recv_b.at[me_p], plane_peer(p))
        copy.start()
        sent.append(copy)
    small.wait_send()
    push(s_a.at[other], s_a.at[other], ssend_a, srecv_a, partner).wait_recv()
    s_b[me_p] = s_a[0] + s_a[1]
    for p in plane_others:
        copy = push(s_b.at[me_p], s_b.at[me_p], ssend_b.at[p], srecv_b.at[me_p], plane_peer(p))
        copy.start()
        sent.append(copy)
    acc2[...] = acc1[me_p]
    for p in plane_others:
        push(b_src.at[p], b_dst.at[p], send_b.at[p], recv_b.at[p], plane_peer(p)).wait_recv()
        acc2[...] += b_dst[p].astype(F32)
    c_src[...] = acc2[...].astype(BF16)

    for r in row_others:
        copy = push(c_src.at[r], c_dst.at[row], send_c.at[r], recv_c.at[row], (mem, r, col))
        copy.start()
        sent.append(copy)
    for p in plane_others:
        push(s_b.at[p], s_b.at[p], ssend_b.at[p], srecv_b.at[p], plane_peer(p)).wait_recv()
    total = s_b[0]
    for p in range(1, planes):
        total = total + s_b[p]
    s_c[row] = total
    for r in row_others:
        copy = push(s_c.at[row], s_c.at[row], ssend_c.at[r], srecv_c.at[row], (mem, r, col))
        copy.start()
        sent.append(copy)
    whole = acc2[row]
    for r in row_others:
        push(c_src.at[r], c_dst.at[r], send_c.at[r], recv_c.at[r], (mem, r, col)).wait_recv()
        whole = whole + c_dst[r].astype(F32)
    gz[row] = (whole * scale).astype(BF16)

    for r in row_others:
        copy = push(gz.at[row], gz.at[row], send_z.at[r], recv_z.at[row], (mem, r, col))
        copy.start()
        sent.append(copy)
    for r in row_others:
        push(s_c.at[r], s_c.at[r], ssend_c.at[r], srecv_c.at[r], (mem, r, col)).wait_recv()
    total = s_c[0]
    for r in range(1, rows):
        total = total + s_c[r]
    sout_ref[...] = total * scale
    for r in row_others:
        push(gz.at[r], gz.at[r], send_z.at[r], recv_z.at[r], (mem, r, col)).wait_recv()
    for p in plane_others:
        copy = push(gz, gp.at[me_p], send_p.at[p], recv_p.at[me_p], plane_peer(p))
        copy.start()
        sent.append(copy)
    own = push(gz, ga.at[me_p], send_g.at[me_p], recv_g.at[me_p], partner)
    own.start()
    sent.append(own)
    out_ref[core, me_p] = gz[...].astype(F32)
    for p in plane_others:
        push(gz, gp.at[p], send_p.at[p], recv_p.at[p], plane_peer(p)).wait_recv()
        copy = push(gp.at[p], ga.at[p], send_g.at[p], recv_g.at[p], partner)
        copy.start()
        sent.append(copy)
        out_ref[core, p] = gp[p].astype(F32)
    for p in [me_p] + plane_others:
        push(gz, ga.at[p], send_g.at[p], recv_g.at[p], partner).wait_recv()
        out_ref[other, p] = ga[p].astype(F32)
    for copy in sent:
        copy.wait_send()


def sum_all(grads, small, scale, collective_id):
    rows, cols = lax.axis_size("row"), lax.axis_size("col")
    planes = lax.axis_size("mem") // 2 * cols
    height, width = grads.shape
    unit = (height // (2 * planes * rows), width)
    part, half = (rows,) + unit, (planes, rows) + unit
    full = (2,) + half
    sems = pltpu.SemaphoreType.DMA
    out, sout = pl.pallas_call(
        functools.partial(sum_kernel, planes, rows, cols, scale),
        out_shape=(jax.ShapeDtypeStruct(full, F32), jax.ShapeDtypeStruct(small.shape, F32)),
        in_specs=[VMEM_SPEC] * 2,
        out_specs=(VMEM_SPEC,) * 2,
        scratch_shapes=[
            pltpu.VMEM(half, BF16), pltpu.VMEM(half, BF16), pltpu.VMEM(half, F32),
            pltpu.VMEM(half, BF16), pltpu.VMEM(half, BF16), pltpu.VMEM(part, F32),
            pltpu.VMEM(part, BF16), pltpu.VMEM(part, BF16), pltpu.VMEM(part, BF16),
            pltpu.VMEM(half, BF16), pltpu.VMEM(half, BF16),
            pltpu.VMEM((2,) + small.shape, F32),
            pltpu.VMEM((planes,) + small.shape, F32),
            pltpu.VMEM((rows,) + small.shape, F32),
            sems(()), sems(()), sems((planes,)), sems((planes,)), sems((rows,)), sems((rows,)),
            sems((rows,)), sems((rows,)), sems((planes,)), sems((planes,)),
            sems((planes,)), sems((planes,)),
            sems((planes,)), sems((planes,)), sems((rows,)), sems((rows,)), sems(()), sems(()),
        ],
        compiler_params=pltpu.CompilerParams(
            collective_id=collective_id, has_side_effects=True, vmem_limit_bytes=48 * 2**20
        ),
    )(grads.reshape(full), small)
    return out.reshape(height, width), sout


def with_halo(x, sides, width):
    for axis, dim in sides:
        size, length = (lax.axis_size(axis), x.shape[dim])
        up = [(i, (i + 1) % size) for i in range(size - 1)]
        down = [(j, i) for i, j in up]
        last = lax.slice_in_dim(x, length - width, length, axis=dim)
        first = lax.slice_in_dim(x, 0, width, axis=dim)
        before = lax.ppermute(last, axis, up)
        after = lax.ppermute(first, axis, down)
        x = jnp.concatenate([before, x, after], axis=dim)
    return x


def local(fields, norm_gain, w_query, w_key, w_value, w_out, mix_kernel, cotangent):
    members, tile_rows, tile_cols, width = fields.shape
    cells = tile_rows * tile_cols
    padded_cot = with_halo(cotangent, (("row", 1), ("col", 2)), 1)
    shifts = [
        padded_cot[:, 2 - i : 2 - i + tile_rows, 2 - j : 2 - j + tile_cols, :].astype(F32)
        for i in range(3)
        for j in range(3)
    ]
    taps = mix_kernel.reshape(9, width)
    summed = jnp.zeros(fields.shape, F32)
    for i in range(9):
        summed = summed + taps[i] * shifts[i]
    count = lax.axis_size("mem")
    split = (members, count, cells // count, width)
    f_got, gm_got = exchange(fields.reshape(split), summed.astype(BF16).reshape(split), True, 1)
    joined = (members * count, cells // count, width)
    corr, mixed, grads, gain = block(
        f_got.reshape(joined), gm_got.reshape(joined), norm_gain, w_query, w_key, w_value, w_out
    )
    sender = (count, members, cells // count, width)
    corr, mixed = exchange(corr.reshape(sender), mixed.reshape(sender), False, 2)
    grad_fields = (cotangent.astype(F32) + corr.reshape(fields.shape).astype(F32)).astype(BF16)
    mixed = mixed.reshape(fields.shape).astype(F32)
    terms = [jnp.sum(s * mixed, axis=(0, 1, 2))[None] for s in shifts]
    small = jnp.concatenate([gain, *terms, jnp.zeros((6, width), F32)])
    tokens = math.prod(fields.shape[:3]) * math.prod(
        lax.axis_size(a) for a in ("mem", "row", "col")
    )
    total, small = sum_all(grads, small, 1.0 / math.sqrt(tokens), 3)
    w = [total[i * width : (i + 1) * width] for i in range(4)]
    return (grad_fields, small[0], *w, small[1:10].reshape(3, 3, width))


def solution(mesh):
    tile = P("mem", "row", "col", None)
    in_specs = (tile, P(), P(), P(), P(), P(), P(), tile)
    out_specs = (tile, P(), P(), P(), P(), P(), P())
    return jax.shard_map(local, mesh=mesh, in_specs=in_specs, out_specs=out_specs, check_vma=False)
```

```python
import functools
import math

import jax
import jax.numpy as jnp
from jax import lax
from jax.experimental import pallas as pl
from jax.experimental.pallas import tpu as pltpu
from jax.sharding import PartitionSpec as P

HEADS = 8
SUB = 8

epsilon = 1e-06
F32 = jnp.float32
BF16 = jnp.bfloat16


def dot_nn(a, b):
    return lax.dot_general(a, b, (((1,), (0,)), ((), ())), preferred_element_type=F32)


def dot_nt(a, b):
    return lax.dot_general(a, b, (((1,), (1,)), ((), ())), preferred_element_type=F32)


def flip(x):
    return x.astype(F32).T.astype(x.dtype)


def to_groups(x):
    members, cells, width = x.shape
    return jnp.concatenate(
        [x[:, i : i + SUB, :].reshape(members * SUB, width) for i in range(0, cells, SUB)], axis=0
    )


def from_groups(x, members, cells):
    width = x.shape[-1]
    size = members * SUB
    return jnp.concatenate(
        [x[g * size : (g + 1) * size].reshape(members, SUB, width) for g in range(cells // SUB)],
        axis=1,
    )


def attend_group(keys, vals, q_t, ga_t, k_t, v_t):
    tokens, width = keys.shape
    members = tokens // SUB
    head_dim = width // HEADS
    scale = 1.0 / math.sqrt(head_dim)
    head_of = lax.broadcasted_iota(jnp.int32, (tokens, width), 1) // head_dim
    row_cell = lax.broadcasted_iota(jnp.int32, (SUB, tokens), 0)
    col_cell = lax.broadcasted_iota(jnp.int32, (SUB, tokens), 1) % SUB
    same = (row_cell == col_cell)[None]
    outs = ([], [], [], [])
    for h in range(HEADS):
        own = head_of == h
        hs = slice(h * head_dim, (h + 1) * head_dim)
        k_own = jnp.where(own, keys.astype(F32), 0.0).astype(BF16)
        v_own = jnp.where(own, vals.astype(F32), 0.0).astype(BF16)
        scores = dot_nn(k_own, q_t).reshape(members, SUB, tokens) * scale
        grad_prob = dot_nn(v_own, ga_t).reshape(members, SUB, tokens)
        lifted = jnp.exp(scores - jnp.max(scores, axis=0, keepdims=True))
        prob = lifted * (1.0 / jnp.sum(lifted, axis=0, keepdims=True))
        inner = jnp.sum(prob * grad_prob, axis=0, keepdims=True)
        grad_score = prob * (grad_prob - inner) * scale
        prob_b = jnp.where(same, prob, 0.0).reshape(tokens, tokens).astype(BF16)
        gs_b = jnp.where(same, grad_score, 0.0).reshape(tokens, tokens).astype(BF16)
        outs[0].append(dot_nn(v_t[hs], prob_b))
        outs[1].append(dot_nn(k_t[hs], gs_b))
        outs[2].append(dot_nt(q_t[hs], gs_b))
        outs[3].append(dot_nt(ga_t[hs], prob_b))
    return tuple(jnp.concatenate(o, axis=0).astype(BF16) for o in outs)


def block_kernel(
    f_ref, gm_ref, gain_ref, wq_ref, wk_ref, wv_ref, wo_ref,
    corr_ref, mixed_ref, grads_ref, gain_out_ref,
):
    members, cells, width = f_ref.shape
    size = members * SUB
    flat = to_groups(f_ref[...].astype(F32))
    gm = to_groups(gm_ref[...].astype(F32)).astype(BF16)
    wq, wk, wv, wo = (w[...] for w in (wq_ref, wk_ref, wv_ref, wo_ref))
    inv = lax.rsqrt(jnp.mean(flat * flat, axis=-1, keepdims=True) + epsilon)
    normed = flat * inv
    inputs = (normed * gain_ref[...]).astype(BF16)
    in_t = flip(inputs)
    keys = dot_nn(inputs, wk).astype(BF16)
    vals = dot_nn(inputs, wv).astype(BF16)
    q_t = dot_nn(flip(wq), in_t).astype(BF16)
    k_t = dot_nn(flip(wk), in_t).astype(BF16)
    v_t = dot_nn(flip(wv), in_t).astype(BF16)
    ga_t = dot_nt(wo, gm).astype(BF16)
    parts = []
    for g in range(cells // SUB):
        rows = slice(g * size, (g + 1) * size)
        parts.append(
            attend_group(
                keys[rows], vals[rows], q_t[:, rows], ga_t[:, rows], k_t[:, rows], v_t[:, rows]
            )
        )
    att_t, gq_t, gk_t, gv_t = (jnp.concatenate(p, axis=1) for p in zip(*parts))
    mixed = dot_nn(flip(att_t), wo)
    mixed_ref[...] = from_groups(mixed, members, cells).astype(BF16)
    grad_in = (dot_nn(wq, gq_t) + dot_nn(wk, gk_t) + dot_nn(wv, gv_t)).T
    grads_ref[0:width] = dot_nt(in_t, gq_t)
    grads_ref[width : 2 * width] = dot_nt(in_t, gk_t)
    grads_ref[2 * width : 3 * width] = dot_nt(in_t, gv_t)
    grads_ref[3 * width : 4 * width] = dot_nn(att_t, gm)
    gain_out_ref[...] = jnp.sum(grad_in * normed, axis=0, keepdims=True)
    grad_normed = grad_in * gain_ref[...]
    corr = inv * (grad_normed - normed * jnp.mean(grad_normed * normed, axis=-1, keepdims=True))
    corr_ref[...] = from_groups(corr, members, cells).astype(BF16)


def block(f, gm, gain, wq, wk, wv, wo, interpret=False):
    width = f.shape[-1]
    return pl.pallas_call(
        block_kernel,
        out_shape=(
            jax.ShapeDtypeStruct(f.shape, BF16),
            jax.ShapeDtypeStruct(f.shape, BF16),
            jax.ShapeDtypeStruct((4 * width, width), F32),
            jax.ShapeDtypeStruct((1, width), F32),
        ),
        interpret=interpret,
        compiler_params=pltpu.CompilerParams(vmem_limit_bytes=48 * 2**20),
    )(f, gm, gain.reshape(1, -1), wq, wk, wv, wo)


MESH = pl.DeviceIdType.MESH
VMEM_SPEC = pl.BlockSpec(memory_space=pltpu.VMEM)


def enter(peers):
    barrier = pltpu.get_barrier_semaphore()
    for peer in peers:
        pl.semaphore_signal(barrier, inc=1, device_id=peer, device_id_type=MESH)
    pl.semaphore_wait(barrier, len(peers))


def push(src, dst, send_sem, recv_sem, peer):
    return pltpu.make_async_remote_copy(
        src_ref=src, dst_ref=dst, send_sem=send_sem, recv_sem=recv_sem,
        device_id=peer, device_id_type=MESH,
    )


def exchange_kernel(count, *refs):
    inward = False
    srcs, dsts, (send, recv) = refs[:2], refs[2:4], refs[4:]
    me = lax.axis_index("mem")
    row, col = lax.axis_index("row"), lax.axis_index("col")
    others = [lax.rem(me + k, count) for k in range(1, count)]
    enter([(o, row, col) for o in others])

    def view(ref, i, by_chunk):
        return ref.at[:, i] if by_chunk else ref.at[i]

    copies = []
    for t in range(2):
        for o in others:
            copy = push(
                view(srcs[t], o, inward), view(dsts[t], me, not inward),
                send.at[t, o], recv.at[t, me], (o, row, col),
            )
            copy.start()
            copies.append(copy)
    for t in range(2):
        if inward:
            dsts[t][me] = srcs[t][:, me]
        else:
            dsts[t][:, me] = srcs[t][me]
    for copy in copies:
        copy.wait_send()
    for t in range(2):
        for o in others:
            push(
                view(srcs[t], o, inward), view(dsts[t], o, not inward),
                send.at[t, o], recv.at[t, o], (o, row, col),
            ).wait_recv()


def exchange(a, b, collective_id):
    count = lax.axis_size("mem")
    shape = a.shape
    out = (shape[1], shape[0]) + shape[2:]
    return pl.pallas_call(
        functools.partial(exchange_kernel, count),
        out_shape=(jax.ShapeDtypeStruct(out, a.dtype),) * 2,
        in_specs=[VMEM_SPEC] * 2,
        out_specs=(VMEM_SPEC,) * 2,
        scratch_shapes=[pltpu.SemaphoreType.DMA((2, count))] * 2,
        compiler_params=pltpu.CompilerParams(collective_id=collective_id, has_side_effects=True),
    )(a, b)


def sum_kernel(
    planes, rows, cols, scale,
    g_ref, s_ref, out_ref, sout_ref,
    a_src, a_dst, acc1, b_src, b_dst, acc2, c_src, c_dst, gz, gp, ga, s_a, s_b, s_c,
    send_a, recv_a, send_b, recv_b, send_c, recv_c,
    send_z, recv_z, send_p, recv_p, send_g, recv_g,
    ssend_b, srecv_b, ssend_c, srecv_c, ssend_a, srecv_a,
):
    mem, row, col = (lax.axis_index(a) for a in ("mem", "row", "col"))
    core = lax.rem(mem, 2)
    other = 1 - core
    me_p = lax.div(mem, 2) * cols + col
    partner = (mem + 1 - 2 * core, row, col)

    def plane_peer(p):
        return (lax.div(p, cols) * 2 + core, row, lax.rem(p, cols))

    plane_others = [lax.rem(me_p + k, planes) for k in range(1, planes)]
    row_others = [lax.rem(row + k, rows) for k in range(1, rows)]
    enter(
        [partner]
        + [plane_peer(p) for p in plane_others]
        + [(mem, r, col) for r in row_others]
    )

    a_src[...] = g_ref[other].astype(BF16)
    first = push(a_src, a_dst, send_a, recv_a, partner)
    first.start()
    s_a[core] = s_ref[...]
    small = push(s_a.at[core], s_a.at[core], ssend_a, srecv_a, partner)
    small.start()
    first.wait()
    acc1[...] = g_ref[core] + a_dst[...].astype(F32)
    b_src[...] = acc1[...].astype(BF16)

    sent = []
    for p in plane_others:
        copy = push(b_src.at[p], b_dst.at[me_p], send_b.at[p], recv_b.at[me_p], plane_peer(p))
        copy.start()
        sent.append(copy)
    small.wait_send()
    push(s_a.at[other], s_a.at[other], ssend_a, srecv_a, partner).wait_recv()
    s_b[me_p] = s_a[0] + s_a[1]
    for p in plane_others:
        copy = push(s_b.at[me_p], s_b.at[me_p], ssend_b.at[p], srecv_b.at[me_p], plane_peer(p))
        copy.start()
        sent.append(copy)
    acc2[...] = acc1[me_p]
    for p in plane_others:
        push(b_src.at[p], b_dst.at[p], send_b.at[p], recv_b.at[p], plane_peer(p)).wait_recv()
        acc2[...] += b_dst[p].astype(F32)
    c_src[...] = acc2[...].astype(BF16)

    for r in row_others:
        copy = push(c_src.at[r], c_dst.at[row], send_c.at[r], recv_c.at[row], (mem, r, col))
        copy.start()
        sent.append(copy)
    for p in plane_others:
        push(s_b.at[p], s_b.at[p], ssend_b.at[p], srecv_b.at[p], plane_peer(p)).wait_recv()
    total = s_b[0]
    for p in range(1, planes):
        total = total + s_b[p]
    s_c[row] = total
    for r in row_others:
        copy = push(s_c.at[row], s_c.at[row], ssend_c.at[r], srecv_c.at[row], (mem, r, col))
        copy.start()
        sent.append(copy)
    whole = acc2[row]
    for r in row_others:
        push(c_src.at[r], c_dst.at[r], send_c.at[r], recv_c.at[r], (mem, r, col)).wait_recv()
        whole = whole + c_dst[r].astype(F32)
    gz[row] = (whole * scale).astype(BF16)

    for r in row_others:
        copy = push(gz.at[row], gz.at[row], send_z.at[r], recv_z.at[row], (mem, r, col))
        copy.start()
        sent.append(copy)
    for r in row_others:
        push(s_c.at[r], s_c.at[r], ssend_c.at[r], srecv_c.at[r], (mem, r, col)).wait_recv()
    total = s_c[0]
    for r in range(1, rows):
        total = total + s_c[r]
    sout_ref[...] = total * scale
    for r in row_others:
        push(gz.at[r], gz.at[r], send_z.at[r], recv_z.at[r], (mem, r, col)).wait_recv()
    for p in plane_others:
        copy = push(gz, gp.at[me_p], send_p.at[p], recv_p.at[me_p], plane_peer(p))
        copy.start()
        sent.append(copy)
    own = push(gz, ga.at[me_p], send_g.at[me_p], recv_g.at[me_p], partner)
    own.start()
    sent.append(own)
    out_ref[core, me_p] = gz[...].astype(F32)
    for p in plane_others:
        push(gz, gp.at[p], send_p.at[p], recv_p.at[p], plane_peer(p)).wait_recv()
        copy = push(gp.at[p], ga.at[p], send_g.at[p], recv_g.at[p], partner)
        copy.start()
        sent.append(copy)
        out_ref[core, p] = gp[p].astype(F32)
    for p in [me_p] + plane_others:
        push(gz, ga.at[p], send_g.at[p], recv_g.at[p], partner).wait_recv()
        out_ref[other, p] = ga[p].astype(F32)
    for copy in sent:
        copy.wait_send()


def sum_all(grads, small, scale, collective_id):
    rows, cols = lax.axis_size("row"), lax.axis_size("col")
    planes = lax.axis_size("mem") // 2 * cols
    height, width = grads.shape
    unit = (height // (2 * planes * rows), width)
    part, half = (rows,) + unit, (planes, rows) + unit
    full = (2,) + half
    sems = pltpu.SemaphoreType.DMA
    out, sout = pl.pallas_call(
        functools.partial(sum_kernel, planes, rows, cols, scale),
        out_shape=(jax.ShapeDtypeStruct(full, F32), jax.ShapeDtypeStruct(small.shape, F32)),
        in_specs=[VMEM_SPEC] * 2,
        out_specs=(VMEM_SPEC,) * 2,
        scratch_shapes=[
            pltpu.VMEM(half, BF16), pltpu.VMEM(half, BF16), pltpu.VMEM(half, F32),
            pltpu.VMEM(half, BF16), pltpu.VMEM(half, BF16), pltpu.VMEM(part, F32),
            pltpu.VMEM(part, BF16), pltpu.VMEM(part, BF16), pltpu.VMEM(part, BF16),
            pltpu.VMEM(half, BF16), pltpu.VMEM(half, BF16),
            pltpu.VMEM((2,) + small.shape, F32),
            pltpu.VMEM((planes,) + small.shape, F32),
            pltpu.VMEM((rows,) + small.shape, F32),
            sems(()), sems(()), sems((planes,)), sems((planes,)), sems((rows,)), sems((rows,)),
            sems((rows,)), sems((rows,)), sems((planes,)), sems((planes,)),
            sems((planes,)), sems((planes,)),
            sems((planes,)), sems((planes,)), sems((rows,)), sems((rows,)), sems(()), sems(()),
        ],
        compiler_params=pltpu.CompilerParams(
            collective_id=collective_id, has_side_effects=True, vmem_limit_bytes=48 * 2**20
        ),
    )(grads.reshape(full), small)
    return out.reshape(height, width), sout

NEAR = [(dr, dc) for dr in (-1, 0, 1) for dc in (-1, 0, 1) if (dr, dc) != (0, 0)]
EDGE = 8


def entry_kernel(
    count, grid,
    f_ref, cot_ref, edges_ref, taps_ref, f_out, gm_out, pad_out,
    row_halo, col_halo, pad, gm_src, send, recv, near_send, near_recv,
):
    members, rows, cols, width = cot_ref.shape
    me = lax.axis_index("mem")
    at = (lax.axis_index("row"), lax.axis_index("col"))
    others = [lax.rem(me + k, count) for k in range(1, count)]

    def exists(step):
        tests = [
            (at[i] > 0) if step[i] < 0 else (at[i] < grid[i] - 1) for i in range(2) if step[i]
        ]
        return functools.reduce(jnp.logical_and, tests)

    def neighbour(step):
        return (me, at[0] + step[0], at[1] + step[1])

    def outgoing(step):
        dr, dc = step
        if dc == 0:
            return cot_ref.at[:, 0 if dr < 0 else rows - 1]
        side = edges_ref.at[0 if dc < 0 else 1]
        return side if dr == 0 else side.at[0 if dr < 0 else rows - 1]

    def landing(step):
        dr, dc = step
        if dc == 0:
            return row_halo.at[0 if dr < 0 else 1]
        side = col_halo.at[0 if dc < 0 else 1]
        return side.at[pl.ds(1, rows)] if dr == 0 else side.at[0 if dr < 0 else rows + 1]

    def halo_copy(i):
        step = NEAR[i]
        back = len(NEAR) - 1 - i
        return push(
            outgoing(step), landing(NEAR[back]), near_send.at[i], near_recv.at[back],
            neighbour(step),
        )

    barrier = pltpu.get_barrier_semaphore()
    for o in others:
        pl.semaphore_signal(barrier, inc=1, device_id=(o, *at), device_id_type=MESH)
    for step in NEAR:
        @pl.when(exists(step))
        def _():
            pl.semaphore_signal(barrier, inc=1, device_id=neighbour(step), device_id_type=MESH)
    present = sum(exists(step).astype(jnp.int32) for step in NEAR)
    pl.semaphore_wait(barrier, present + len(others))

    for i in range(len(NEAR)):
        @pl.when(exists(NEAR[i]))
        def _():
            halo_copy(i).start()

        @pl.when(jnp.logical_not(exists(NEAR[i])))
        def _():
            there = landing(NEAR[i])
            there[...] = jnp.zeros(there.shape, BF16)
    srcs, dsts = (f_ref, gm_src), (f_out, gm_out)

    def spread(t):
        copies = []
        for o in others:
            copy = push(
                srcs[t].at[:, o], dsts[t].at[me], send.at[t, o], recv.at[t, me], (o, *at)
            )
            copy.start()
            copies.append(copy)
        dsts[t][me] = srcs[t][:, me]
        return copies

    copies = spread(0)
    pad[:, 1 : rows + 1, EDGE : EDGE + cols, :] = cot_ref[...].astype(F32)
    for i in range(len(NEAR)):
        @pl.when(exists(NEAR[i]))
        def _():
            there = landing(NEAR[i])
            push(
                there, there, near_send.at[i], near_recv.at[i], neighbour(NEAR[i])
            ).wait_recv()
    pad[:, 0, EDGE : EDGE + cols, :] = row_halo[0].astype(F32)
    pad[:, rows + 1, EDGE : EDGE + cols, :] = row_halo[1].astype(F32)
    for side, place in ((0, EDGE - 1), (1, EDGE + cols)):
        for r in range(rows + 2):
            column = col_halo[side, r].astype(F32)
            for m in range(members):
                pad[m, r, place : place + 1, :] = column[m : m + 1]
    for m in range(members):
        summed = jnp.zeros((rows, cols, width), F32)
        for i in range(3):
            for j in range(3):
                first = EDGE + 1 - j
                summed = summed + taps_ref[3 * i + j : 3 * i + j + 1, :] * pad[
                    m, 2 - i : 2 - i + rows, first : first + cols, :
                ]
        gm_src[m] = summed.reshape(gm_src.shape[1:]).astype(BF16)
    copies += spread(1)
    pad_out[...] = pad[:, :, EDGE - 1 : EDGE + 1 + cols, :].astype(BF16)
    for i in range(len(NEAR)):
        @pl.when(exists(NEAR[i]))
        def _():
            halo_copy(i).wait_send()
    for copy in copies:
        copy.wait_send()
    for t in range(2):
        for o in others:
            push(
                srcs[t].at[:, o], dsts[t].at[o], send.at[t, o], recv.at[t, o], (o, *at)
            ).wait_recv()


def entry(fields, cotangent, taps, collective_id):
    count = lax.axis_size("mem")
    members, rows, cols, width = fields.shape
    cells = rows * cols // count
    split = (members, count, cells, width)
    got = (count, members, cells, width)
    edges = jnp.swapaxes(jnp.stack([cotangent[:, :, 0], cotangent[:, :, -1]]), 1, 2)
    sems = pltpu.SemaphoreType.DMA
    return pl.pallas_call(
        functools.partial(entry_kernel, count, (lax.axis_size("row"), lax.axis_size("col"))),
        out_shape=(
            jax.ShapeDtypeStruct(got, BF16),
            jax.ShapeDtypeStruct(got, BF16),
            jax.ShapeDtypeStruct((members, rows + 2, cols + 2, width), BF16),
        ),
        in_specs=[VMEM_SPEC] * 4,
        out_specs=(VMEM_SPEC,) * 3,
        scratch_shapes=[
            pltpu.VMEM((2, members, cols, width), BF16),
            pltpu.VMEM((2, rows + 2, members, width), BF16),
            pltpu.VMEM((members, rows + 2, cols + 2 * EDGE, width), F32),
            pltpu.VMEM(split, BF16),
            sems((2, count)), sems((2, count)), sems((len(NEAR),)), sems((len(NEAR),)),
        ],
        compiler_params=pltpu.CompilerParams(
            collective_id=collective_id, has_side_effects=True, vmem_limit_bytes=48 * 2**20
        ),
    )(fields.reshape(split), cotangent, edges, taps)


def local(fields, norm_gain, w_query, w_key, w_value, w_out, mix_kernel, cotangent):
    members, tile_rows, tile_cols, width = fields.shape
    cells = tile_rows * tile_cols
    count = lax.axis_size("mem")
    f_got, gm_got, padded_cot = entry(fields, cotangent, mix_kernel.reshape(9, width), 1)
    shifts = [
        padded_cot[:, 2 - i : 2 - i + tile_rows, 2 - j : 2 - j + tile_cols, :].astype(F32)
        for i in range(3)
        for j in range(3)
    ]
    joined = (members * count, cells // count, width)
    corr, mixed, grads, gain = block(
        f_got.reshape(joined), gm_got.reshape(joined), norm_gain, w_query, w_key, w_value, w_out
    )
    sender = (count, members, cells // count, width)
    corr, mixed = exchange(corr.reshape(sender), mixed.reshape(sender), 2)
    grad_fields = (cotangent.astype(F32) + corr.reshape(fields.shape).astype(F32)).astype(BF16)
    mixed = mixed.reshape(fields.shape).astype(F32)
    terms = [jnp.sum(s * mixed, axis=(0, 1, 2))[None] for s in shifts]
    small = jnp.concatenate([gain, *terms, jnp.zeros((6, width), F32)])
    tokens = math.prod(fields.shape[:3]) * math.prod(
        lax.axis_size(a) for a in ("mem", "row", "col")
    )
    total, small = sum_all(grads, small, 1.0 / math.sqrt(tokens), 3)
    w = [total[i * width : (i + 1) * width] for i in range(4)]
    return (grad_fields, small[0], *w, small[1:10].reshape(3, 3, width))


def solution(mesh):
    tile = P("mem", "row", "col", None)
    in_specs = (tile, P(), P(), P(), P(), P(), P(), tile)
    out_specs = (tile, P(), P(), P(), P(), P(), P())
    return jax.shard_map(local, mesh=mesh, in_specs=in_specs, out_specs=out_specs, check_vma=False)
```

```python
import functools
import math

import jax
import jax.numpy as jnp
from jax import lax
from jax.experimental import pallas as pl
from jax.experimental.pallas import tpu as pltpu
from jax.sharding import PartitionSpec as P

HEADS = 8
SUB = 8

epsilon = 1e-06
F32 = jnp.float32
BF16 = jnp.bfloat16


def dot_nn(a, b):
    return lax.dot_general(a, b, (((1,), (0,)), ((), ())), preferred_element_type=F32)


def dot_nt(a, b):
    return lax.dot_general(a, b, (((1,), (1,)), ((), ())), preferred_element_type=F32)


def flip(x):
    return x.astype(F32).T.astype(x.dtype)


def to_groups(x):
    members, cells, width = x.shape
    return jnp.concatenate(
        [x[:, i : i + SUB, :].reshape(members * SUB, width) for i in range(0, cells, SUB)], axis=0
    )


def from_groups(x, members, cells):
    width = x.shape[-1]
    size = members * SUB
    return jnp.concatenate(
        [x[g * size : (g + 1) * size].reshape(members, SUB, width) for g in range(cells // SUB)],
        axis=1,
    )


def attend_group(keys, vals, q_t, ga_t, k_t, v_t):
    tokens, width = keys.shape
    members = tokens // SUB
    head_dim = width // HEADS
    scale = 1.0 / math.sqrt(head_dim)
    head_of = lax.broadcasted_iota(jnp.int32, (tokens, width), 1) // head_dim
    row_cell = lax.broadcasted_iota(jnp.int32, (SUB, tokens), 0)
    col_cell = lax.broadcasted_iota(jnp.int32, (SUB, tokens), 1) % SUB
    same = (row_cell == col_cell)[None]
    outs = ([], [], [], [])
    for h in range(HEADS):
        own = head_of == h
        hs = slice(h * head_dim, (h + 1) * head_dim)
        k_own = jnp.where(own, keys.astype(F32), 0.0).astype(BF16)
        v_own = jnp.where(own, vals.astype(F32), 0.0).astype(BF16)
        scores = dot_nn(k_own, q_t).reshape(members, SUB, tokens) * scale
        grad_prob = dot_nn(v_own, ga_t).reshape(members, SUB, tokens)
        lifted = jnp.exp(scores - jnp.max(scores, axis=0, keepdims=True))
        prob = lifted * (1.0 / jnp.sum(lifted, axis=0, keepdims=True))
        inner = jnp.sum(prob * grad_prob, axis=0, keepdims=True)
        grad_score = prob * (grad_prob - inner) * scale
        prob_b = jnp.where(same, prob, 0.0).reshape(tokens, tokens).astype(BF16)
        gs_b = jnp.where(same, grad_score, 0.0).reshape(tokens, tokens).astype(BF16)
        outs[0].append(dot_nn(v_t[hs], prob_b))
        outs[1].append(dot_nn(k_t[hs], gs_b))
        outs[2].append(dot_nt(q_t[hs], gs_b))
        outs[3].append(dot_nt(ga_t[hs], prob_b))
    return tuple(jnp.concatenate(o, axis=0).astype(BF16) for o in outs)


def block_kernel(
    f_ref, gm_ref, gain_ref, wq_ref, wk_ref, wv_ref, wo_ref,
    corr_ref, mixed_ref, grads_ref, gain_out_ref,
):
    members, cells, width = f_ref.shape
    size = members * SUB
    flat = to_groups(f_ref[...].astype(F32))
    gm = to_groups(gm_ref[...].astype(F32)).astype(BF16)
    wq, wk, wv, wo = (w[...] for w in (wq_ref, wk_ref, wv_ref, wo_ref))
    inv = lax.rsqrt(jnp.mean(flat * flat, axis=-1, keepdims=True) + epsilon)
    normed = flat * inv
    inputs = (normed * gain_ref[...]).astype(BF16)
    in_t = flip(inputs)
    keys = dot_nn(inputs, wk).astype(BF16)
    vals = dot_nn(inputs, wv).astype(BF16)
    q_t = dot_nn(flip(wq), in_t).astype(BF16)
    k_t = dot_nn(flip(wk), in_t).astype(BF16)
    v_t = dot_nn(flip(wv), in_t).astype(BF16)
    ga_t = dot_nt(wo, gm).astype(BF16)
    parts = []
    for g in range(cells // SUB):
        rows = slice(g * size, (g + 1) * size)
        parts.append(
            attend_group(
                keys[rows], vals[rows], q_t[:, rows], ga_t[:, rows], k_t[:, rows], v_t[:, rows]
            )
        )
    att_t, gq_t, gk_t, gv_t = (jnp.concatenate(p, axis=1) for p in zip(*parts))
    mixed = dot_nn(flip(att_t), wo)
    mixed_ref[...] = from_groups(mixed, members, cells).astype(BF16)
    grad_in = (dot_nn(wq, gq_t) + dot_nn(wk, gk_t) + dot_nn(wv, gv_t)).T
    grads_ref[0:width] = dot_nt(in_t, gq_t)
    grads_ref[width : 2 * width] = dot_nt(in_t, gk_t)
    grads_ref[2 * width : 3 * width] = dot_nt(in_t, gv_t)
    grads_ref[3 * width : 4 * width] = dot_nn(att_t, gm)
    gain_out_ref[...] = jnp.sum(grad_in * normed, axis=0, keepdims=True)
    grad_normed = grad_in * gain_ref[...]
    corr = inv * (grad_normed - normed * jnp.mean(grad_normed * normed, axis=-1, keepdims=True))
    corr_ref[...] = from_groups(corr, members, cells).astype(BF16)


def block(f, gm, gain, wq, wk, wv, wo, interpret=False):
    width = f.shape[-1]
    return pl.pallas_call(
        block_kernel,
        out_shape=(
            jax.ShapeDtypeStruct(f.shape, BF16),
            jax.ShapeDtypeStruct(f.shape, BF16),
            jax.ShapeDtypeStruct((4 * width, width), F32),
            jax.ShapeDtypeStruct((1, width), F32),
        ),
        interpret=interpret,
        compiler_params=pltpu.CompilerParams(vmem_limit_bytes=48 * 2**20),
    )(f, gm, gain.reshape(1, -1), wq, wk, wv, wo)


MESH = pl.DeviceIdType.MESH
VMEM_SPEC = pl.BlockSpec(memory_space=pltpu.VMEM)


def enter(peers):
    barrier = pltpu.get_barrier_semaphore()
    for peer in peers:
        pl.semaphore_signal(barrier, inc=1, device_id=peer, device_id_type=MESH)
    pl.semaphore_wait(barrier, len(peers))


def push(src, dst, send_sem, recv_sem, peer):
    return pltpu.make_async_remote_copy(
        src_ref=src, dst_ref=dst, send_sem=send_sem, recv_sem=recv_sem,
        device_id=peer, device_id_type=MESH,
    )


def exchange_kernel(count, src, dst, send, recv):
    me = lax.axis_index("mem")
    row, col = lax.axis_index("row"), lax.axis_index("col")
    others = [lax.rem(me + k, count) for k in range(1, count)]
    enter([(o, row, col) for o in others])

    copies, arrivals = exchange_start(src, dst, send, recv, me, others, (row, col))
    exchange_finish(copies, arrivals)


def exchange_start(src, dst, send, recv, me, others, place):
    copies, arrivals = [], []
    for o in others:
        copy = push(src.at[o], dst.at[:, me], send.at[o], recv.at[me], (o, *place))
        copy.start()
        copies.append(copy)
        arrivals.append(push(src.at[o], dst.at[:, o], send.at[o], recv.at[o], (o, *place)))
    dst[:, me] = src[me]
    return copies, arrivals


def exchange_finish(copies, arrivals):
    for copy in copies:
        copy.wait_send()
    for arrival in arrivals:
        arrival.wait_recv()


def exchange(a, collective_id):
    count = lax.axis_size("mem")
    shape = a.shape
    out = (shape[1], shape[0]) + shape[2:]
    return pl.pallas_call(
        functools.partial(exchange_kernel, count),
        out_shape=jax.ShapeDtypeStruct(out, a.dtype),
        in_specs=[VMEM_SPEC],
        out_specs=VMEM_SPEC,
        scratch_shapes=[pltpu.SemaphoreType.DMA((count,))] * 2,
        compiler_params=pltpu.CompilerParams(collective_id=collective_id, has_side_effects=True),
    )(a)


def sum_kernel(
    count, planes, rows, cols, scale,
    g_ref, s_ref, x_ref, out_ref, sout_ref, x_out,
    a_src, a_dst, acc1, b_src, b_dst, acc2, c_src, c_dst, gz, gp, ga, s_a, s_b, s_c,
    send_a, recv_a, send_b, recv_b, send_c, recv_c,
    send_z, recv_z, send_p, recv_p, send_g, recv_g,
    ssend_b, srecv_b, ssend_c, srecv_c, ssend_a, srecv_a, xsend, xrecv,
):
    mem, row, col = (lax.axis_index(a) for a in ("mem", "row", "col"))
    core = lax.rem(mem, 2)
    other = 1 - core
    me_p = lax.div(mem, 2) * cols + col
    partner = (mem + 1 - 2 * core, row, col)

    def plane_peer(p):
        return (lax.div(p, cols) * 2 + core, row, lax.rem(p, cols))

    plane_others = [lax.rem(me_p + k, planes) for k in range(1, planes)]
    row_others = [lax.rem(row + k, rows) for k in range(1, rows)]
    mem_others = [lax.rem(mem + k, count) for k in range(1, count)]
    enter(
        [(o, row, col) for o in mem_others]
        + [partner]
        + [plane_peer(p) for p in plane_others]
        + [(mem, r, col) for r in row_others]
    )

    a_src[...] = g_ref[other].astype(BF16)
    first = push(a_src, a_dst, send_a, recv_a, partner)
    first.start()
    s_a[core] = s_ref[...]
    small = push(s_a.at[core], s_a.at[core], ssend_a, srecv_a, partner)
    small.start()
    moving = exchange_start(x_ref, x_out, xsend, xrecv, mem, mem_others, (row, col))
    first.wait()
    acc1[...] = g_ref[core] + a_dst[...].astype(F32)
    b_src[...] = acc1[...].astype(BF16)

    sent = []
    for p in plane_others:
        copy = push(b_src.at[p], b_dst.at[me_p], send_b.at[p], recv_b.at[me_p], plane_peer(p))
        copy.start()
        sent.append(copy)
    small.wait_send()
    push(s_a.at[other], s_a.at[other], ssend_a, srecv_a, partner).wait_recv()
    s_b[me_p] = s_a[0] + s_a[1]
    for p in plane_others:
        copy = push(s_b.at[me_p], s_b.at[me_p], ssend_b.at[p], srecv_b.at[me_p], plane_peer(p))
        copy.start()
        sent.append(copy)
    acc2[...] = acc1[me_p]
    for p in plane_others:
        push(b_src.at[p], b_dst.at[p], send_b.at[p], recv_b.at[p], plane_peer(p)).wait_recv()
        acc2[...] += b_dst[p].astype(F32)
    c_src[...] = acc2[...].astype(BF16)

    for r in row_others:
        copy = push(c_src.at[r], c_dst.at[row], send_c.at[r], recv_c.at[row], (mem, r, col))
        copy.start()
        sent.append(copy)
    for p in plane_others:
        push(s_b.at[p], s_b.at[p], ssend_b.at[p], srecv_b.at[p], plane_peer(p)).wait_recv()
    total = s_b[0]
    for p in range(1, planes):
        total = total + s_b[p]
    s_c[row] = total
    for r in row_others:
        copy = push(s_c.at[row], s_c.at[row], ssend_c.at[r], srecv_c.at[row], (mem, r, col))
        copy.start()
        sent.append(copy)
    whole = acc2[row]
    for r in row_others:
        push(c_src.at[r], c_dst.at[r], send_c.at[r], recv_c.at[r], (mem, r, col)).wait_recv()
        whole = whole + c_dst[r].astype(F32)
    gz[row] = (whole * scale).astype(BF16)

    for r in row_others:
        copy = push(gz.at[row], gz.at[row], send_z.at[r], recv_z.at[row], (mem, r, col))
        copy.start()
        sent.append(copy)
    for r in row_others:
        push(s_c.at[r], s_c.at[r], ssend_c.at[r], srecv_c.at[r], (mem, r, col)).wait_recv()
    total = s_c[0]
    for r in range(1, rows):
        total = total + s_c[r]
    sout_ref[...] = total * scale
    for r in row_others:
        push(gz.at[r], gz.at[r], send_z.at[r], recv_z.at[r], (mem, r, col)).wait_recv()
    for p in plane_others:
        copy = push(gz, gp.at[me_p], send_p.at[p], recv_p.at[me_p], plane_peer(p))
        copy.start()
        sent.append(copy)
    own = push(gz, ga.at[me_p], send_g.at[me_p], recv_g.at[me_p], partner)
    own.start()
    sent.append(own)
    out_ref[core, me_p] = gz[...].astype(F32)
    for p in plane_others:
        push(gz, gp.at[p], send_p.at[p], recv_p.at[p], plane_peer(p)).wait_recv()
        copy = push(gp.at[p], ga.at[p], send_g.at[p], recv_g.at[p], partner)
        copy.start()
        sent.append(copy)
        out_ref[core, p] = gp[p].astype(F32)
    for p in [me_p] + plane_others:
        push(gz, ga.at[p], send_g.at[p], recv_g.at[p], partner).wait_recv()
        out_ref[other, p] = ga[p].astype(F32)
    for copy in sent:
        copy.wait_send()
    exchange_finish(*moving)


def sum_all(grads, small, x, scale, collective_id):
    count = lax.axis_size("mem")
    x_shape = (x.shape[1], x.shape[0]) + x.shape[2:]
    rows, cols = lax.axis_size("row"), lax.axis_size("col")
    planes = lax.axis_size("mem") // 2 * cols
    height, width = grads.shape
    unit = (height // (2 * planes * rows), width)
    part, half = (rows,) + unit, (planes, rows) + unit
    full = (2,) + half
    sems = pltpu.SemaphoreType.DMA
    out, sout, x = pl.pallas_call(
        functools.partial(sum_kernel, count, planes, rows, cols, scale),
        out_shape=(
            jax.ShapeDtypeStruct(full, F32),
            jax.ShapeDtypeStruct(small.shape, F32),
            jax.ShapeDtypeStruct(x_shape, x.dtype),
        ),
        in_specs=[VMEM_SPEC] * 3,
        out_specs=(VMEM_SPEC,) * 3,
        scratch_shapes=[
            pltpu.VMEM(half, BF16), pltpu.VMEM(half, BF16), pltpu.VMEM(half, F32),
            pltpu.VMEM(half, BF16), pltpu.VMEM(half, BF16), pltpu.VMEM(part, F32),
            pltpu.VMEM(part, BF16), pltpu.VMEM(part, BF16), pltpu.VMEM(part, BF16),
            pltpu.VMEM(half, BF16), pltpu.VMEM(half, BF16),
            pltpu.VMEM((2,) + small.shape, F32),
            pltpu.VMEM((planes,) + small.shape, F32),
            pltpu.VMEM((rows,) + small.shape, F32),
            sems(()), sems(()), sems((planes,)), sems((planes,)), sems((rows,)), sems((rows,)),
            sems((rows,)), sems((rows,)), sems((planes,)), sems((planes,)),
            sems((planes,)), sems((planes,)),
            sems((planes,)), sems((planes,)), sems((rows,)), sems((rows,)), sems(()), sems(()),
            sems((count,)), sems((count,)),
        ],
        compiler_params=pltpu.CompilerParams(
            collective_id=collective_id, has_side_effects=True, vmem_limit_bytes=48 * 2**20
        ),
    )(grads.reshape(full), small, x)
    return out.reshape(height, width), sout, x

NEAR = [(dr, dc) for dr in (-1, 0, 1) for dc in (-1, 0, 1) if (dr, dc) != (0, 0)]
EDGE = 8


def entry_kernel(
    count, grid,
    f_ref, cot_ref, edges_ref, taps_ref, f_out, gm_out, pad_out,
    row_halo, col_halo, pad, gm_src, send, recv, near_send, near_recv,
):
    members, rows, cols, width = cot_ref.shape
    me = lax.axis_index("mem")
    at = (lax.axis_index("row"), lax.axis_index("col"))
    others = [lax.rem(me + k, count) for k in range(1, count)]

    def exists(step):
        tests = [
            (at[i] > 0) if step[i] < 0 else (at[i] < grid[i] - 1) for i in range(2) if step[i]
        ]
        return functools.reduce(jnp.logical_and, tests)

    def neighbour(step):
        return (me, at[0] + step[0], at[1] + step[1])

    def outgoing(step):
        dr, dc = step
        if dc == 0:
            return cot_ref.at[:, 0 if dr < 0 else rows - 1]
        side = edges_ref.at[0 if dc < 0 else 1]
        return side if dr == 0 else side.at[0 if dr < 0 else rows - 1]

    def landing(step):
        dr, dc = step
        if dc == 0:
            return row_halo.at[0 if dr < 0 else 1]
        side = col_halo.at[0 if dc < 0 else 1]
        return side.at[pl.ds(1, rows)] if dr == 0 else side.at[0 if dr < 0 else rows + 1]

    def halo_copy(i):
        step = NEAR[i]
        back = len(NEAR) - 1 - i
        return push(
            outgoing(step), landing(NEAR[back]), near_send.at[i], near_recv.at[back],
            neighbour(step),
        )

    barrier = pltpu.get_barrier_semaphore()
    for o in others:
        pl.semaphore_signal(barrier, inc=1, device_id=(o, *at), device_id_type=MESH)
    for step in NEAR:
        @pl.when(exists(step))
        def _():
            pl.semaphore_signal(barrier, inc=1, device_id=neighbour(step), device_id_type=MESH)
    present = sum(exists(step).astype(jnp.int32) for step in NEAR)
    pl.semaphore_wait(barrier, present + len(others))

    for i in range(len(NEAR)):
        @pl.when(exists(NEAR[i]))
        def _():
            halo_copy(i).start()

        @pl.when(jnp.logical_not(exists(NEAR[i])))
        def _():
            there = landing(NEAR[i])
            there[...] = jnp.zeros(there.shape, BF16)
    srcs, dsts = (f_ref, gm_src), (f_out, gm_out)

    def spread(t):
        copies = []
        for o in others:
            copy = push(
                srcs[t].at[:, o], dsts[t].at[me], send.at[t, o], recv.at[t, me], (o, *at)
            )
            copy.start()
            copies.append(copy)
        dsts[t][me] = srcs[t][:, me]
        return copies

    copies = spread(0)
    pad[:, 1 : rows + 1, EDGE : EDGE + cols, :] = cot_ref[...].astype(F32)
    for i in range(len(NEAR)):
        @pl.when(exists(NEAR[i]))
        def _():
            there = landing(NEAR[i])
            push(
                there, there, near_send.at[i], near_recv.at[i], neighbour(NEAR[i])
            ).wait_recv()
    pad[:, 0, EDGE : EDGE + cols, :] = row_halo[0].astype(F32)
    pad[:, rows + 1, EDGE : EDGE + cols, :] = row_halo[1].astype(F32)
    for side, place in ((0, EDGE - 1), (1, EDGE + cols)):
        for r in range(rows + 2):
            column = col_halo[side, r].astype(F32)
            for m in range(members):
                pad[m, r, place : place + 1, :] = column[m : m + 1]
    for m in range(members):
        summed = jnp.zeros((rows, cols, width), F32)
        for i in range(3):
            for j in range(3):
                first = EDGE + 1 - j
                summed = summed + taps_ref[3 * i + j : 3 * i + j + 1, :] * pad[
                    m, 2 - i : 2 - i + rows, first : first + cols, :
                ]
        gm_src[m] = summed.reshape(gm_src.shape[1:]).astype(BF16)
    copies += spread(1)
    pad_out[...] = pad[:, :, EDGE - 1 : EDGE + 1 + cols, :].astype(BF16)
    for i in range(len(NEAR)):
        @pl.when(exists(NEAR[i]))
        def _():
            halo_copy(i).wait_send()
    for copy in copies:
        copy.wait_send()
    for t in range(2):
        for o in others:
            push(
                srcs[t].at[:, o], dsts[t].at[o], send.at[t, o], recv.at[t, o], (o, *at)
            ).wait_recv()


def entry(fields, cotangent, taps, collective_id):
    count = lax.axis_size("mem")
    members, rows, cols, width = fields.shape
    cells = rows * cols // count
    split = (members, count, cells, width)
    got = (count, members, cells, width)
    edges = jnp.swapaxes(jnp.stack([cotangent[:, :, 0], cotangent[:, :, -1]]), 1, 2)
    sems = pltpu.SemaphoreType.DMA
    return pl.pallas_call(
        functools.partial(entry_kernel, count, (lax.axis_size("row"), lax.axis_size("col"))),
        out_shape=(
            jax.ShapeDtypeStruct(got, BF16),
            jax.ShapeDtypeStruct(got, BF16),
            jax.ShapeDtypeStruct((members, rows + 2, cols + 2, width), BF16),
        ),
        in_specs=[VMEM_SPEC] * 4,
        out_specs=(VMEM_SPEC,) * 3,
        scratch_shapes=[
            pltpu.VMEM((2, members, cols, width), BF16),
            pltpu.VMEM((2, rows + 2, members, width), BF16),
            pltpu.VMEM((members, rows + 2, cols + 2 * EDGE, width), F32),
            pltpu.VMEM(split, BF16),
            sems((2, count)), sems((2, count)), sems((len(NEAR),)), sems((len(NEAR),)),
        ],
        compiler_params=pltpu.CompilerParams(
            collective_id=collective_id, has_side_effects=True, vmem_limit_bytes=48 * 2**20
        ),
    )(fields.reshape(split), cotangent, edges, taps)


def local(fields, norm_gain, w_query, w_key, w_value, w_out, mix_kernel, cotangent):
    members, tile_rows, tile_cols, width = fields.shape
    cells = tile_rows * tile_cols
    count = lax.axis_size("mem")
    f_got, gm_got, padded_cot = entry(fields, cotangent, mix_kernel.reshape(9, width), 1)
    shifts = [
        padded_cot[:, 2 - i : 2 - i + tile_rows, 2 - j : 2 - j + tile_cols, :].astype(F32)
        for i in range(3)
        for j in range(3)
    ]
    joined = (members * count, cells // count, width)
    corr, mixed, grads, gain = block(
        f_got.reshape(joined), gm_got.reshape(joined), norm_gain, w_query, w_key, w_value, w_out
    )
    sender = (count, members, cells // count, width)
    mixed = exchange(mixed.reshape(sender), 2)
    mixed = mixed.reshape(fields.shape).astype(F32)
    terms = [jnp.sum(s * mixed, axis=(0, 1, 2))[None] for s in shifts]
    small = jnp.concatenate([gain, *terms, jnp.zeros((6, width), F32)])
    tokens = math.prod(fields.shape[:3]) * math.prod(
        lax.axis_size(a) for a in ("mem", "row", "col")
    )
    total, small, corr = sum_all(grads, small, corr.reshape(sender), 1.0 / math.sqrt(tokens), 3)
    grad_fields = (cotangent.astype(F32) + corr.reshape(fields.shape).astype(F32)).astype(BF16)
    w = [total[i * width : (i + 1) * width] for i in range(4)]
    return (grad_fields, small[0], *w, small[1:10].reshape(3, 3, width))


def solution(mesh):
    tile = P("mem", "row", "col", None)
    in_specs = (tile, P(), P(), P(), P(), P(), P(), tile)
    out_specs = (tile, P(), P(), P(), P(), P(), P())
    return jax.shard_map(local, mesh=mesh, in_specs=in_specs, out_specs=out_specs, check_vma=False)
```
